768 devices in a mesh: pipe: 24 (over x_lo, z), zero: 32 (over y, x_hi, core).
Axes of the slice: x: 4 (x_hi: 2, x_lo: 2; x = x_hi * 2 + x_lo), y: 8, z: 12, core: 2. Of those that a mesh axis runs over, the one named last changes fastest.
Arguments:
- down_out: bfloat16 [24, 256, 2048], P('pipe', 'zero'), may hold values from -6 to 6
- up_out: bfloat16 [24, 256, 2048], P('pipe', 'zero'), may hold values from -6 to 6
- feeds: bfloat16 [2, 256, 2048], P(None, 'zero'), may hold values from -6 to 6
- order: int32 [2], replicated, may hold values from 0 to 1, each once
- gains: float32 [24, 2, 2048], P('pipe'), may hold values from 0.1 to 1.9
- gate_w: bfloat16 [24, 2, 2048, 4096], P('pipe', None, None, 'zero'), may hold values from -0.125 to 0.125
- up_w: bfloat16 [24, 2, 2048, 4096], P('pipe', None, None, 'zero'), may hold values from -0.125 to 0.125
- down_w: bfloat16 [24, 2, 4096, 2048], P('pipe', None, 'zero'), may hold values from -0.09375 to 0.09375
Outputs:
- down_next: bfloat16 [24, 256, 2048], P('pipe', 'zero')
- up_next: bfloat16 [24, 256, 2048], P('pipe', 'zero')
The draws below stay inside these ranges and needn't reach their ends.
Inputs may be any that keep to these rules, and one draw needn't show every extreme that they name: `order`: every micro-batch index enters exactly once.
All inputs are finite; a program needn't handle non-finite values.
Results may differ from the reference program's by a relative error of at most 0.02.
Values may be sent and summed in bfloat16 or wider, within the bound.
A program may use at most 32 MiB of HBM per device.

```python
import jax
import jax.numpy as jnp
from jax import lax

D = 2048
FF = 4096
TICKS = 2
SECTIONS = 24
MB = 256
N_ZERO = 32


def steps_of(rng, dims, cuts, least, largest):
    loudness, own = 1.0, jax.random.fold_in(rng, 6)
    for position, parts in cuts:
        draws = jnp.exp(jax.random.uniform(jax.random.fold_in(own, position), (parts,), jnp.float32, least / len(cuts), largest / len(cuts)))
        loudness = loudness * jnp.repeat(draws, dims[position] // parts).reshape([-1 if axis == position else 1 for axis in range(len(dims))])
    return loudness


def normal_values(own_key, extent, spread, reach, cuts=(), held_as=jnp.bfloat16):
    drawn = jax.random.normal(own_key, extent, jnp.float32) * spread
    if len(cuts) > 0:
        drawn = steps_of(own_key, extent, cuts, -0.22, 0.18) * drawn
    return jnp.clip(drawn, min=-reach, max=reach).astype(held_as)


def setup_inputs(seed: int = 0) -> dict:
    splits = jax.random.split(jax.random.key(seed), 9)
    down_out = normal_values(splits[0], (SECTIONS, MB, D), 1.0, 6.0, ((0, 24), (1, 32)))
    up_out = normal_values(splits[1], (SECTIONS, MB, D), 1.0, 6.0, ((0, 24), (1, 32)))
    feeds = normal_values(splits[2], (TICKS, MB, D), 1.0, 6.0, ((1, 32),))
    order = jax.random.permutation(splits[3], TICKS).astype(jnp.int32)
    gains = jnp.clip(1.0 + 0.18 * jax.random.normal(splits[4], (SECTIONS, 2, D), jnp.float32), 0.1, 1.9)
    gate_w = normal_values(splits[5], (SECTIONS, 2, D, FF), D ** -0.5, 0.125, ((0, 24), (3, 32)))
    up_w = normal_values(splits[6], (SECTIONS, 2, D, FF), D ** -0.5, 0.125, ((0, 24), (3, 32)))
    down_w = normal_values(splits[7], (SECTIONS, 2, FF, D), FF ** -0.5, 0.09375, ((0, 24), (2, 32)))
    return dict(down_out=down_out, up_out=up_out, feeds=feeds, order=order, gains=gains, gate_w=gate_w, up_w=up_w, down_w=down_w)


def group(x, gain, w_gate, w_up, w_down):
    xf = x.astype(jnp.float32)
    normed = (xf * lax.rsqrt(lax.optimization_barrier(jnp.mean(xf * xf, axis=-1, keepdims=True)) + 1e-05) * gain).astype(jnp.bfloat16)
    gate = jnp.dot(normed, w_gate, preferred_element_type=jnp.float32)
    up = jnp.dot(normed, w_up, preferred_element_type=jnp.float32)
    hidden = (jax.nn.silu(gate) * up).astype(jnp.bfloat16)
    rows = hidden.shape[0]
    width = hidden.shape[1] // N_ZERO
    blocks = hidden.reshape(rows, N_ZERO, width).astype(jnp.float32)
    weights = w_down.reshape(N_ZERO, width, w_down.shape[1]).astype(jnp.float32)
    partial_value = jnp.einsum('mnf,nfd->nmd', blocks, weights).astype(jnp.bfloat16)
    summed = lax.optimization_barrier(jnp.sum(partial_value.astype(jnp.float32), axis=0))
    return (xf + summed).astype(jnp.bfloat16)

def section_pair(items):
    down_in, up_in, gain_pair, gate_pair, up_pair, down_pair = items
    first = group(down_in, gain_pair[0], gate_pair[0], up_pair[0], down_pair[0])
    second = group(up_in, gain_pair[1], gate_pair[1], up_pair[1], down_pair[1])
    return (first, second)

def reference(down_out, up_out, feeds, order, gains, gate_w, up_w, down_w):
    down_next = down_out
    up_next = up_out
    for tick in range(TICKS):
        entering = feeds[order[tick]]
        down_in = jnp.concatenate([entering[None], down_next[:-1]], axis=0)
        up_in = jnp.concatenate([up_next[1:], down_next[-1:]], axis=0)
        down_next, up_next = lax.map(section_pair, (down_in, up_in, gains, gate_w, up_w, down_w))
    return (down_next, up_next)
```

```python
import functools

import jax
import jax.numpy as jnp
from jax import lax
from jax.experimental import pallas as pl
from jax.experimental.pallas import tpu as pltpu
from jax.sharding import PartitionSpec as P

MESH = pl.DeviceIdType.MESH
TICKS = 2
RING = 8
ROWS = 8

SLOTS = (
    (0, 0), (1, 0), (0, 1), (0, 7),
    (0, 2), (0, 6), (1, 1), (1, 7),
    (0, 3), (0, 5), (1, 2), (1, 6),
    (0, 4), (1, 3), (1, 5), (1, 4),
)
SLOT = {pair: index for index, pair in enumerate(SLOTS)}
UP_REACH = (4, 3)

GATHER = {}
REDUCE = {}
count = 0
for b, d in SLOTS[1:]:
    GATHER[b, d] = count
    count += 1
PAIR_GATHER = count
count += 16
PAIR_REDUCE = count
count += 4
for b in range(2):
    for way in range(2):
        reach = UP_REACH[b] if way == 0 else 7 - UP_REACH[b]
        for hop in range(reach):
            REDUCE[b, way, hop] = count
            count += 1
CROSS = count
SHIFT = count + 1
COPIES = count + 2


def kernel(n_pipe, down_ref, up_ref, feeds_ref, order_ref, gains_ref, gate_ref, upw_ref, downw_ref,
           out_down, out_up,
           wgu, wd, gain_v, feed_v, local_v, xin, xs, ag, part, pair_out, pair_in, run_out, run_in, cross_out, cross_in,
           y_buf, send_sem, recv_sem, load_sem):
    p = lax.axis_index("pipe")
    q = lax.axis_index("zero")
    d_model = wgu.shape[1]
    ahead = (p, lax.rem(q + 4, 32))
    behind = (p, lax.rem(q + 28, 32))
    across = (p, q + 2 - 4 * lax.rem(q // 2, 2))
    partner = (p, q + 1 - 2 * lax.rem(q, 2))
    later = (lax.rem(p + 1, n_pipe), q)
    earlier = (lax.rem(p + n_pipe - 1, n_pipe), q)

    loads = []

    def load(src, dst):
        copy = pltpu.make_async_copy(src, dst, load_sem.at[len(loads)])
        copy.start()
        loads.append(copy)

    load(feeds_ref, feed_v)
    load(down_ref, local_v)
    load(gains_ref, gain_v)
    for g in range(2):
        load(gate_ref.at[0, g], wgu.at[g, :, pl.ds(0, 128)])
        load(upw_ref.at[0, g], wgu.at[g, :, pl.ds(128, 128)])
        load(downw_ref.at[0, g], wd.at[g])

    barrier = pltpu.get_barrier_semaphore()
    for device in (ahead, behind, across, partner, later, earlier):
        pl.semaphore_signal(barrier, inc=1, device_id=device, device_id_type=MESH)
    pl.semaphore_wait(barrier, 6)

    def remote(t, g, number, src, dst, device):
        index = (t * 2 + g) * COPIES + number
        return pltpu.make_async_remote_copy(
            src_ref=src, dst_ref=dst, send_sem=send_sem.at[index], recv_sem=recv_sem.at[index],
            device_id=device, device_id_type=MESH)

    sent = []

    def send(*args):
        copy = remote(*args)
        copy.start()
        sent.append(copy)

    def arrive(t, g, number, dst):
        remote(t, g, number, dst, dst, partner).wait_recv()

    def place(t, g, b, d, r=0):
        return ag.at[t, g, r, SLOT[b, d]]

    def pass_on(t, g, b, d):
        src = place(t, g, b, d)
        if d == 0:
            if b == 0:
                send(t, g, GATHER[1, 0], src, place(t, g, 1, 0), across)
            send(t, g, GATHER[b, 1], src, place(t, g, b, 1), ahead)
            send(t, g, GATHER[b, 7], src, place(t, g, b, 7), behind)
        elif d < UP_REACH[b]:
            send(t, g, GATHER[b, d + 1], src, place(t, g, b, d + 1), ahead)
        elif d > UP_REACH[b] + 1:
            send(t, g, GATHER[b, d - 1], src, place(t, g, b, d - 1), behind)
        send(t, g, PAIR_GATHER + SLOT[b, d], src, place(t, g, b, d, 1), partner)

    def take(t, g, b, d):
        arrive(t, g, GATHER[b, d], place(t, g, b, d))
        pass_on(t, g, b, d)

    def begin(t, g):
        arrive(t, g, SHIFT, xin.at[t, g])
        arrived = xin[t, g].astype(jnp.float32)
        if g == 0:
            x = jnp.where(p == 0, feed_v[order_ref[t]].astype(jnp.float32), arrived)
        else:
            own = local_v[0] if t == 0 else y_buf[0, 0]
            x = jnp.where(p == n_pipe - 1, own.astype(jnp.float32), arrived)
        xs[t, g] = x.astype(jnp.bfloat16)
        scale = lax.rsqrt(jnp.mean(x * x, axis=-1, keepdims=True) + 1e-05)
        ag[t, g, 0, 0] = (x * scale * gain_v[0, pl.ds(g, 1), :]).astype(jnp.bfloat16)
        pass_on(t, g, 0, 0)

    def multiply(t, g, chunk):
        first = chunk * 4
        for k in range(first, first + 4):
            arrive(t, g, PAIR_GATHER + k, ag.at[t, g, 1, k])
        rows = ag[t, g, :, pl.ds(first, 4)].astype(jnp.float32).reshape(64, d_model).astype(jnp.bfloat16)
        both = jnp.dot(rows, wgu[g], preferred_element_type=jnp.float32)
        gate = both[:, :128]
        hidden = (gate / (1.0 + jnp.exp(-gate)) * both[:, 128:]).astype(jnp.bfloat16)
        width = min(512, d_model)
        for n in range(d_model // width):
            cols = pl.ds(n * width, width)
            product = jnp.dot(hidden, wd[g, :, cols], preferred_element_type=jnp.float32)
            product = product.reshape(2, 4, ROWS, width).astype(jnp.bfloat16)
            part[t, g, pl.ds(first, 4), :, cols] = product[0]
            pair_out[t, g, pl.ds(first, 4), :, cols] = product[1]
        send(t, g, PAIR_REDUCE + chunk, pair_out.at[t, g, pl.ds(first, 4)], pair_in.at[t, g, pl.ds(first, 4)], partner)

    def paired(t, g, chunk):
        arrive(t, g, PAIR_REDUCE + chunk, pair_in.at[t, g, pl.ds(chunk * 4, 4)])

    def own_sum(t, g, b, d):
        k = SLOT[b, d]
        return part[t, g, k].astype(jnp.float32) + pair_in[t, g, k].astype(jnp.float32)

    def run_slot(b, way, hop):
        return REDUCE[b, way, hop] - REDUCE[0, 0, 0]

    def reach_of(b, way):
        return UP_REACH[b] if way == 0 else 7 - UP_REACH[b]

    def distance(b, way, hop):
        return (8 - UP_REACH[b] + hop) if way == 0 else (7 - UP_REACH[b] - hop)

    def relay(t, g, b, way, hop):
        total = own_sum(t, g, b, distance(b, way, hop))
        if hop > 0:
            slot = run_slot(b, way, hop - 1)
            arrive(t, g, REDUCE[b, way, hop - 1], run_in.at[t, g, slot])
            total = total + run_in[t, g, slot].astype(jnp.float32)
        slot = run_slot(b, way, hop)
        run_out[t, g, slot] = total.astype(jnp.bfloat16)
        send(t, g, REDUCE[b, way, hop], run_out.at[t, g, slot], run_in.at[t, g, slot], ahead if way == 0 else behind)

    def gathered_sum(t, g, b):
        total = own_sum(t, g, b, 0)
        for way in range(2):
            hop = reach_of(b, way) - 1
            slot = run_slot(b, way, hop)
            arrive(t, g, REDUCE[b, way, hop], run_in.at[t, g, slot])
            total = total + run_in[t, g, slot].astype(jnp.float32)
        return total

    def cross(t, g):
        cross_out[t, g] = gathered_sum(t, g, 1).astype(jnp.bfloat16)
        send(t, g, CROSS, cross_out.at[t, g], cross_in.at[t, g], across)

    def finish(t, g):
        total = gathered_sum(t, g, 0)
        arrive(t, g, CROSS, cross_in.at[t, g])
        total = total + cross_in[t, g].astype(jnp.float32)
        y = (xs[t, g].astype(jnp.float32) + total).astype(jnp.bfloat16)
        if t + 1 < TICKS:
            y_buf[t, g] = y
            send(t + 1, g, SHIFT, y_buf.at[t, g], xin.at[t + 1, g], later if g == 0 else earlier)
        elif g == 0:
            out_down[0] = y
        else:
            out_up[0] = y

    send(0, 0, SHIFT, down_ref.at[0], xin.at[0, 0], later)
    send(0, 1, SHIFT, up_ref.at[0], xin.at[0, 1], earlier)
    for copy in loads[:3]:
        copy.wait()
    for t in range(TICKS):
        for g in range(2):
            begin(t, g)
        for stage, blocks in enumerate((
            ((0, 1), (0, 7)), ((1, 0),), ((0, 2), (0, 6)), ((1, 1), (1, 7)),
            ((0, 3), (0, 5)), ((1, 2), (1, 6)), ((0, 4),), ((1, 3), (1, 5)), ((1, 4),),
        )):
            for g in range(2):
                for b, d in blocks:
                    take(t, g, b, d)
            if t == 0 and stage == 2:
                for copy in loads[3:]:
                    copy.wait()
            if stage in (3, 5, 7):
                for g in range(2):
                    multiply(t, g, (stage - 3) // 2)
        for g in range(2):
            for chunk in range(3):
                paired(t, g, chunk)
            relay(t, g, 0, 1, 0)
        for g in range(2):
            multiply(t, g, 3)
        for g in range(2):
            paired(t, g, 3)
            relay(t, g, 1, 1, 0)
            relay(t, g, 1, 0, 0)
            relay(t, g, 0, 0, 0)
        for hop in range(1, 4):
            for g in range(2):
                for b, way in ((1, 1), (1, 0), (0, 0), (0, 1)):
                    if hop < reach_of(b, way):
                        relay(t, g, b, way, hop)
        for g in range(2):
            cross(t, g)
        for g in range(2):
            finish(t, g)
    for copy in sent:
        copy.wait_send()


def solution(mesh):
    n_pipe = mesh.shape["pipe"]

    def on_device(down_out, up_out, feeds, order, gains, gate_w, up_w, down_w):
        d_model = down_out.shape[-1]
        half = jnp.bfloat16
        block = jax.ShapeDtypeStruct((1, ROWS, d_model), half)
        anywhere = pl.BlockSpec(memory_space=pl.ANY)
        vmem = pl.BlockSpec(memory_space=pltpu.VMEM)
        runs = (TICKS, 2)
        return pl.pallas_call(
            functools.partial(kernel, n_pipe),
            out_shape=(block, block),
            in_specs=[anywhere] * 3 + [pl.BlockSpec(memory_space=pltpu.SMEM)] + [anywhere] * 4,
            out_specs=(vmem, vmem),
            scratch_shapes=[
                pltpu.VMEM((2, d_model, 256), half),
                pltpu.VMEM((2, 128, d_model), half),
                pltpu.VMEM((1, 2, d_model), jnp.float32),
                pltpu.VMEM((TICKS, ROWS, d_model), half),
                pltpu.VMEM((1, ROWS, d_model), half),
                pltpu.VMEM(runs + (ROWS, d_model), half),
                pltpu.VMEM(runs + (ROWS, d_model), half),
                pltpu.VMEM(runs + (2, 16, ROWS, d_model), half),
                pltpu.VMEM(runs + (16, ROWS, d_model), half),
                pltpu.VMEM(runs + (16, ROWS, d_model), half),
                pltpu.VMEM(runs + (16, ROWS, d_model), half),
                pltpu.VMEM(runs + (14, ROWS, d_model), half),
                pltpu.VMEM(runs + (14, ROWS, d_model), half),
                pltpu.VMEM(runs + (ROWS, d_model), half),
                pltpu.VMEM(runs + (ROWS, d_model), half),
                pltpu.VMEM((TICKS - 1, 2, ROWS, d_model), half),
                pltpu.SemaphoreType.DMA((TICKS * 2 * COPIES,)),
                pltpu.SemaphoreType.DMA((TICKS * 2 * COPIES,)),
                pltpu.SemaphoreType.DMA((9,)),
            ],
            compiler_params=pltpu.CompilerParams(
                collective_id=0, has_side_effects=True, vmem_limit_bytes=60 * 1024 * 1024),
        )(down_out, up_out, feeds, order, gains, gate_w, up_w, down_w)

    return jax.shard_map(
        on_device,
        mesh=mesh,
        in_specs=(
            P("pipe", "zero", None),
            P("pipe", "zero", None),
            P(None, "zero", None),
            P(),
            P("pipe", None, None),
            P("pipe", None, None, "zero"),
            P("pipe", None, None, "zero"),
            P("pipe", None, "zero", None),
        ),
        out_specs=(P("pipe", "zero", None), P("pipe", "zero", None)),
        check_vma=False,
    )
```

```python
import functools

import jax
import jax.numpy as jnp
from jax import lax
from jax.experimental import pallas as pl
from jax.experimental.pallas import tpu as pltpu
from jax.sharding import PartitionSpec as P

MESH = pl.DeviceIdType.MESH
TICKS = 2
ROWS = 8

BLOCKS = (
    (0, 0), (0, 1), (0, 7), (0, 2), (0, 6), (1, 0),
    (0, 3), (0, 5), (1, 2), (1, 6), (1, 1),
    (1, 7), (0, 4), (1, 3), (1, 5), (1, 4),
)
CHUNKS = ((0, 6), (6, 5), (11, 5))
SLOT = {block: index for index, block in enumerate(BLOCKS)}
PARENT = {
    (0, 2): (0, 0), (0, 6): (0, 0), (1, 0): (0, 0), (0, 1): (0, 0), (0, 7): (0, 0),
    (1, 3): (0, 2), (0, 4): (0, 2), (1, 2): (0, 2), (0, 3): (0, 2),
    (1, 4): (0, 6), (1, 5): (0, 6), (1, 6): (0, 6), (0, 5): (0, 6),
    (1, 1): (1, 0), (1, 7): (1, 0),
}
CHILDREN = {block: [child for child, parent in PARENT.items() if parent == block] for block in BLOCKS}
RELAYS = [block for block in BLOCKS[1:] if CHILDREN[block]]
LEAVES = [block for block in BLOCKS[1:] if not CHILDREN[block]]

PAIR_GATHER = 16
PAIR_REDUCE = 19
REDUCE = 22
SUMS = {block: REDUCE + index for index, block in enumerate([(0, 0)] + RELAYS)}
ARRIVALS = REDUCE + len(SUMS)
RELAYED, PAIRED, PARTIALS, SUMMED, LAUNCHED, SHIFTED = range(6)
KINDS = 6


def step_of(child, parent):
    return child[0] ^ parent[0], (child[1] - parent[1] + 4) % 8 - 4


def kernel(n_pipe, down_ref, up_ref, feeds_ref, order_ref, gains_ref, gate_ref, upw_ref, downw_ref,
           out_down, out_up,
           wgu, wd, gain_v, feed_v, first, ag, part, pair_out, pair_in, run_out, run_in, y_buf,
           send_sem, recv_sem, load_sem):
    scope = jax.named_scope
    p = lax.axis_index("pipe")
    q = lax.axis_index("zero")
    d_model = wgu.shape[1]
    opposite = q + 2 - 4 * lax.rem(q // 2, 2)

    def device(plane, flip, steps):
        return (plane, lax.rem((opposite if flip else q) + 4 * (steps % 8), 32))

    partner = (p, q + 1 - 2 * lax.rem(q, 2))
    is_first = p == 0
    is_last = p == n_pipe - 1
    stays = (is_last, is_first)

    loads = []

    def load(src, dst):
        copy = pltpu.make_async_copy(src, dst, load_sem.at[len(loads)])
        copy.start()
        loads.append(copy)

    load(feeds_ref, feed_v)
    load(down_ref.at[0], first.at[0])
    load(up_ref.at[0], first.at[1])
    load(gains_ref, gain_v)
    for g in range(2):
        load(gate_ref.at[0, g], wgu.at[g, :, pl.ds(0, 128)])
        load(upw_ref.at[0, g], wgu.at[g, :, pl.ds(128, 128)])
        load(downw_ref.at[0, g], wd.at[g])

    barrier = pltpu.get_barrier_semaphore()
    near = {step_of(child, parent) for child, parent in PARENT.items()}
    near = sorted(near | {(flip, -steps) for flip, steps in near})
    roots = sorted({(0, 0)} | {step_of(child, (0, 0)) for child in CHILDREN[0, 0]})
    meets = [partner] + [device(p, *step) for step in near]
    barrier_count = len(meets) + jnp.where(is_first, 0, len(roots)) + jnp.where(is_last, 0, len(roots))
    with scope("barr"):
        for other in meets:
            pl.semaphore_signal(barrier, inc=1, device_id=other, device_id_type=MESH)

        @pl.when(jnp.logical_not(is_last))
        def _():
            for step in roots:
                pl.semaphore_signal(barrier, inc=1, device_id=device(p + 1, *step), device_id_type=MESH)

        @pl.when(jnp.logical_not(is_first))
        def _():
            for step in roots:
                pl.semaphore_signal(barrier, inc=1, device_id=device(p - 1, *step), device_id_type=MESH)

        pl.semaphore_wait(barrier, barrier_count)

    def leaving(t, g, kind):
        return send_sem.at[(t * 2 + g) * KINDS + kind]

    def arriving(t, g, number):
        return recv_sem.at[(t * 2 + g) * ARRIVALS + number]

    def remote(src, dst, out_sem, in_sem, device):
        return pltpu.make_async_remote_copy(
            src_ref=src, dst_ref=dst, send_sem=out_sem, recv_sem=in_sem, device_id=device, device_id_type=MESH)

    def arrive(t, g, number, dst):
        remote(dst, dst, leaving(t, g, 0), arriving(t, g, number), partner).wait_recv()

    def place(t, g, block, r=0):
        return ag.at[t, g, r, SLOT[block]]

    def launch(t, stream, src, plane, g, stays):
        for child in CHILDREN[0, 0][:2] + [(0, 0)] + CHILDREN[0, 0][2:]:
            kind = SHIFTED if child == (0, 0) else LAUNCHED
            copy = remote(src, place(t, g, child), leaving(t, stream, kind), arriving(t, g, SLOT[child]),
                          device(plane, *step_of(child, (0, 0))))
            if child == (0, 0):
                pl.when(jnp.logical_not(stays))(copy.start)
                own = pltpu.make_async_copy(src, place(t, g, child), arriving(t, g, SLOT[child]))
                pl.when(stays)(own.start)
            else:
                copy.start()

    def launch_down(t, src):
        launch(t, 0, src, jnp.where(is_last, p, p + 1), jnp.where(is_last, 1, 0), is_last)

        @pl.when(is_first)
        def _():
            y_buf[t, 1] = feed_v[order_ref[t]]
            launch(t, 1, y_buf.at[t, 1], p, 0, is_first)

    def launch_up(t, src):
        @pl.when(jnp.logical_not(is_first))
        def _():
            launch(t, 1, src, p - 1, 1, is_first)

    def take(t, g, block):
        src = place(t, g, block)
        arrive(t, g, SLOT[block], src)
        if block != (0, 0):
            for child in CHILDREN[block]:
                remote(src, place(t, g, child), leaving(t, g, RELAYED), arriving(t, g, SLOT[child]),
                       device(p, *step_of(child, block))).start()
        chunk = sum(SLOT[block] >= begin for begin, _ in CHUNKS) - 1
        remote(src, place(t, g, block, 1), leaving(t, g, PAIRED), arriving(t, g, PAIR_GATHER + chunk), partner).start()

    def multiply(t, g, chunk):
        begin, number = CHUNKS[chunk]
        slots = pl.ds(begin, number)
        arrive(t, g, PAIR_GATHER + chunk, ag.at[t, g, 1, slots])
        x = ag[t, g, :, slots].astype(jnp.float32).reshape(2 * number * ROWS, d_model)
        scale = lax.rsqrt(jnp.mean(x * x, axis=-1, keepdims=True) + 1e-05)
        rows = (x * scale * gain_v[0, pl.ds(g, 1), :]).astype(jnp.bfloat16)
        both = jnp.dot(rows, wgu[g], preferred_element_type=jnp.float32)
        gate = both[:, :128]
        hidden = (gate / (1.0 + jnp.exp(-gate)) * both[:, 128:]).astype(jnp.bfloat16)
        width = min(512, d_model)
        for n in range(d_model // width):
            cols = pl.ds(n * width, width)
            product = jnp.dot(hidden, wd[g, :, cols], preferred_element_type=jnp.float32)
            product = product.reshape(2, number, ROWS, width).astype(jnp.bfloat16)
            part[t, g, slots, :, cols] = product[0]
            pair_out[t, g, slots, :, cols] = product[1]
        remote(pair_out.at[t, g, slots], pair_in.at[t, g, slots], leaving(t, g, PARTIALS),
               arriving(t, g, PAIR_REDUCE + chunk), partner).start()

    def total_of(t, g, block):
        k = SLOT[block]
        total = part[t, g, k].astype(jnp.float32) + pair_in[t, g, k].astype(jnp.float32)
        children = CHILDREN[block]
        if children:
            arrive(t, g, SUMS[block], run_in.at[t, g, pl.ds(0, len(children))])
        for child in children:
            total = total + run_in[t, g, SLOT[child]].astype(jnp.float32)
        return total

    def hand_in(t, g, block):
        k = SLOT[block]
        run_out[t, g, k] = total_of(t, g, block).astype(jnp.bfloat16)
        parent = PARENT[block]
        flip, steps = step_of(block, parent)
        remote(run_out.at[t, g, k], run_in.at[t, g, k], leaving(t, g, SUMMED), arriving(t, g, SUMS[parent]),
               device(p, flip, -steps)).start()

    def finish(t, g):
        y = (ag[t, g, 0, 0].astype(jnp.float32) + total_of(t, g, (0, 0))).astype(jnp.bfloat16)
        if t + 1 == TICKS:
            (out_down if g == 0 else out_up)[0] = y
            return
        if g == 0:
            y_buf[t + 1, 0] = y
            launch_down(t + 1, y_buf.at[t + 1, 0])
        else:
            @pl.when(jnp.logical_not(is_first))
            def _():
                y_buf[t + 1, 1] = y
                launch_up(t + 1, y_buf.at[t + 1, 1])

    def enter(t, g):
        with scope(f"L1_{t}{g}"):
            for block in ((0, 2), (0, 6), (1, 0), (0, 0), (0, 1), (0, 7)):
                take(t, g, block)

    def deepen(t, g):
        with scope(f"L2_{t}{g}"):
            for block in BLOCKS[6:]:
                take(t, g, block)

    def work(t, g, chunk):
        with scope(f"M{chunk}_{t}{g}"):
            multiply(t, g, chunk)

    def leaf(t, g, chunk):
        with scope(f"LV{chunk}_{t}{g}"):
            begin, number = CHUNKS[chunk]
            arrive(t, g, PAIR_REDUCE + chunk, pair_in.at[t, g, pl.ds(begin, number)])
            for block in BLOCKS[begin:begin + number]:
                if block in LEAVES:
                    hand_in(t, g, block)

    def relay(t, g):
        with scope(f"RL_{t}{g}"):
            for block in RELAYS:
                hand_in(t, g, block)

    def close(t, g):
        with scope(f"FI_{t}{g}"):
            finish(t, g)

    def start(g):
        with scope(f"GO_{g}"):
            if g == 0:
                launch_down(0, first.at[0])
            else:
                launch_up(0, first.at[1])

    for copy in loads[:3]:
        copy.wait()
    start(0)
    start(1)
    for t in range(TICKS):
        enter(t, 0)
        enter(t, 1)
        if t == 0:
            for copy in loads[3:]:
                copy.wait()
        work(t, 0, 0)
        deepen(t, 0)
        work(t, 1, 0)
        work(t, 0, 1)
        deepen(t, 1)
        work(t, 0, 2)
        leaf(t, 0, 1)
        work(t, 1, 1)
        leaf(t, 0, 2)
        leaf(t, 0, 0)
        work(t, 1, 2)
        leaf(t, 1, 1)
        leaf(t, 1, 0)
        leaf(t, 1, 2)
        relay(t, 0)
        relay(t, 1)
        close(t, 0)
        close(t, 1)
    with scope("drain"):
        for t in range(TICKS):
            for g in range(2):
                for kind, blocks in ((RELAYED, 10), (PAIRED, 16), (PARTIALS, 16), (SUMMED, 15), (LAUNCHED, 5)):
                    ref = ag.at[t, g, 0, pl.ds(0, blocks)]
                    remote(ref, ref, leaving(t, g, kind), arriving(t, g, 0), partner).wait_send()
                ref = ag.at[t, g, 0, 0]
                shift = remote(ref, ref, leaving(t, g, SHIFTED), arriving(t, g, 0), partner)
                pl.when(jnp.logical_not(stays[g]))(shift.wait_send)


def solution(mesh):
    n_pipe = mesh.shape["pipe"]

    def on_device(down_out, up_out, feeds, order, gains, gate_w, up_w, down_w):
        d_model = down_out.shape[-1]
        half = jnp.bfloat16
        block = jax.ShapeDtypeStruct((1, ROWS, d_model), half)
        anywhere = pl.BlockSpec(memory_space=pl.ANY)
        vmem = pl.BlockSpec(memory_space=pltpu.VMEM)
        runs = (TICKS, 2)
        return pl.pallas_call(
            functools.partial(kernel, n_pipe),
            out_shape=(block, block),
            in_specs=[anywhere] * 3 + [pl.BlockSpec(memory_space=pltpu.SMEM)] + [anywhere] * 4,
            out_specs=(vmem, vmem),
            scratch_shapes=[
                pltpu.VMEM((2, d_model, 256), half),
                pltpu.VMEM((2, 128, d_model), half),
                pltpu.VMEM((1, 2, d_model), jnp.float32),
                pltpu.VMEM((TICKS, ROWS, d_model), half),
                pltpu.VMEM((2, ROWS, d_model), half),
                pltpu.VMEM(runs + (2, 16, ROWS, d_model), half),
                pltpu.VMEM(runs + (16, ROWS, d_model), half),
                pltpu.VMEM(runs + (16, ROWS, d_model), half),
                pltpu.VMEM(runs + (16, ROWS, d_model), half),
                pltpu.VMEM(runs + (16, ROWS, d_model), half),
                pltpu.VMEM(runs + (16, ROWS, d_model), half),
                pltpu.VMEM(runs + (ROWS, d_model), half),
                pltpu.SemaphoreType.DMA((TICKS * 2 * KINDS,)),
                pltpu.SemaphoreType.DMA((TICKS * 2 * ARRIVALS,)),
                pltpu.SemaphoreType.DMA((10,)),
            ],
            compiler_params=pltpu.CompilerParams(
                collective_id=0, has_side_effects=True, vmem_limit_bytes=60 * 1024 * 1024),
        )(down_out, up_out, feeds, order, gains, gate_w, up_w, down_w)

    return jax.shard_map(
        on_device,
        mesh=mesh,
        in_specs=(
            P("pipe", "zero", None),
            P("pipe", "zero", None),
            P(None, "zero", None),
            P(),
            P("pipe", None, None),
            P("pipe", None, None, "zero"),
            P("pipe", None, None, "zero"),
            P("pipe", None, "zero", None),
        ),
        out_specs=(P("pipe", "zero", None), P("pipe", "zero", None)),
        check_vma=False,
    )
```

```python
import functools

import jax
import jax.numpy as jnp
from jax import lax
from jax.experimental import pallas as pl
from jax.experimental.pallas import tpu as pltpu
from jax.sharding import PartitionSpec as P

MESH = pl.DeviceIdType.MESH
TICKS = 2
ROWS = 8

BLOCKS = (
    (0, 0), (0, 1), (0, 7), (0, 2), (0, 6), (1, 0),
    (0, 3), (0, 5), (1, 2), (1, 6), (1, 1),
    (1, 7), (0, 4), (1, 3), (1, 5), (1, 4),
)
CHUNKS = ((0, 6), (6, 10))
SLOT = {block: index for index, block in enumerate(BLOCKS)}
PARENT = {
    (0, 2): (0, 0), (0, 6): (0, 0), (1, 0): (0, 0), (0, 1): (0, 0), (0, 7): (0, 0),
    (1, 3): (0, 2), (0, 4): (0, 2), (1, 2): (0, 2), (0, 3): (0, 2),
    (1, 4): (0, 6), (1, 5): (0, 6), (1, 6): (0, 6), (0, 5): (0, 6),
    (1, 1): (1, 0), (1, 7): (1, 0),
}
CHILDREN = {block: [child for child, parent in PARENT.items() if parent == block] for block in BLOCKS}
RELAYS = [block for block in BLOCKS[1:] if CHILDREN[block]]
LEAVES = [block for block in BLOCKS[1:] if not CHILDREN[block]]

PAIR_GATHER = 16
PAIR_REDUCE = 18
REDUCE = 20
SUMS = {block: REDUCE + index for index, block in enumerate([(0, 0)] + RELAYS)}
ARRIVALS = REDUCE + len(SUMS)
RELAYED, PAIRED, PARTIALS, SUMMED, LAUNCHED, SHIFTED = range(6)
KINDS = 6


def step_of(child, parent):
    return child[0] ^ parent[0], (child[1] - parent[1] + 4) % 8 - 4


def kernel(n_pipe, down_ref, up_ref, feeds_ref, order_hbm, gains_ref, gate_ref, upw_ref, downw_ref,
           outs,
           wgu, wd, gain_v, feed_v, first, ag, part, pair_out, pair_in, run_out, run_in, y_buf,
           order_ref, out_v, send_sem, recv_sem, load_sem, store_sem):
    scope = jax.named_scope
    p = lax.axis_index("pipe")
    q = lax.axis_index("zero")
    d_model = wgu.shape[1]
    opposite = q + 2 - 4 * lax.rem(q // 2, 2)

    def device(plane, flip, steps):
        return (plane, lax.rem((opposite if flip else q) + 4 * (steps % 8), 32))

    partner = (p, q + 1 - 2 * lax.rem(q, 2))
    is_first = p == 0
    is_last = p == n_pipe - 1
    stays = (is_last, is_first)

    loads = []

    def load(src, dst):
        copy = pltpu.make_async_copy(src, dst, load_sem.at[len(loads)])
        copy.start()
        loads.append(copy)

    load(order_hbm, order_ref)
    load(feeds_ref, feed_v)
    load(down_ref.at[0], first.at[0])
    load(up_ref.at[0], first.at[1])
    load(gains_ref, gain_v)
    for g in range(2):
        load(gate_ref.at[0, g], wgu.at[g, :, pl.ds(0, 128)])
        load(upw_ref.at[0, g], wgu.at[g, :, pl.ds(128, 128)])
        load(downw_ref.at[0, g], wd.at[g])

    barrier = pltpu.get_barrier_semaphore()
    near = {step_of(child, parent) for child, parent in PARENT.items()}
    near = sorted(near | {(flip, -steps) for flip, steps in near})
    roots = sorted({(0, 0)} | {step_of(child, (0, 0)) for child in CHILDREN[0, 0]})
    meets = [partner] + [device(p, *step) for step in near]
    barrier_count = len(meets) + jnp.where(is_first, 0, len(roots)) + jnp.where(is_last, 0, len(roots))
    with scope("barr"):
        for other in meets:
            pl.semaphore_signal(barrier, inc=1, device_id=other, device_id_type=MESH)

        @pl.when(jnp.logical_not(is_last))
        def _():
            for step in roots:
                pl.semaphore_signal(barrier, inc=1, device_id=device(p + 1, *step), device_id_type=MESH)

        @pl.when(jnp.logical_not(is_first))
        def _():
            for step in roots:
                pl.semaphore_signal(barrier, inc=1, device_id=device(p - 1, *step), device_id_type=MESH)

        pl.semaphore_wait(barrier, barrier_count)

    def leaving(t, g, kind):
        return send_sem.at[(t * 2 + g) * KINDS + kind]

    def arriving(t, g, number):
        return recv_sem.at[(t * 2 + g) * ARRIVALS + number]

    def remote(src, dst, out_sem, in_sem, device):
        return pltpu.make_async_remote_copy(
            src_ref=src, dst_ref=dst, send_sem=out_sem, recv_sem=in_sem, device_id=device, device_id_type=MESH)

    def arrive(t, g, number, dst):
        remote(dst, dst, leaving(t, g, 0), arriving(t, g, number), partner).wait_recv()

    def place(t, g, block, r=0):
        return ag.at[t, g, r, SLOT[block]]

    def launch(t, stream, src, plane, g, stays):
        for child in CHILDREN[0, 0][:2] + [(0, 0)] + CHILDREN[0, 0][2:]:
            kind = SHIFTED if child == (0, 0) else LAUNCHED
            copy = remote(src, place(t, g, child), leaving(t, stream, kind), arriving(t, g, SLOT[child]),
                          device(plane, *step_of(child, (0, 0))))
            if child == (0, 0):
                pl.when(jnp.logical_not(stays))(copy.start)
                own = pltpu.make_async_copy(src, place(t, g, child), arriving(t, g, SLOT[child]))
                pl.when(stays)(own.start)
            else:
                copy.start()

    def launch_down(t, src):
        launch(t, 0, src, jnp.where(is_last, p, p + 1), jnp.where(is_last, 1, 0), is_last)

        @pl.when(is_first)
        def _():
            y_buf[t, 1] = feed_v[order_ref[t]]
            launch(t, 1, y_buf.at[t, 1], p, 0, is_first)

    def launch_up(t, src):
        @pl.when(jnp.logical_not(is_first))
        def _():
            launch(t, 1, src, p - 1, 1, is_first)

    def take(t, g, block):
        src = place(t, g, block)
        arrive(t, g, SLOT[block], src)
        if block != (0, 0):
            for child in CHILDREN[block]:
                remote(src, place(t, g, child), leaving(t, g, RELAYED), arriving(t, g, SLOT[child]),
                       device(p, *step_of(child, block))).start()
        chunk = sum(SLOT[block] >= begin for begin, _ in CHUNKS) - 1
        remote(src, place(t, g, block, 1), leaving(t, g, PAIRED), arriving(t, g, PAIR_GATHER + chunk), partner).start()

    def multiply(t, g, chunk):
        begin, number = CHUNKS[chunk]
        slots = pl.ds(begin, number)
        arrive(t, g, PAIR_GATHER + chunk, ag.at[t, g, 1, slots])
        x = ag[t, g, :, slots].astype(jnp.float32).reshape(2 * number * ROWS, d_model)
        scale = lax.rsqrt(jnp.mean(x * x, axis=-1, keepdims=True) + 1e-05)
        rows = (x * scale * gain_v[0, pl.ds(g, 1), :]).astype(jnp.bfloat16)
        both = jnp.dot(rows, wgu[g], preferred_element_type=jnp.float32)
        gate = both[:, :128]
        hidden = (gate / (1.0 + jnp.exp(-gate)) * both[:, 128:]).astype(jnp.bfloat16)
        width = min(512, d_model)
        for n in range(d_model // width):
            cols = pl.ds(n * width, width)
            product = jnp.dot(hidden, wd[g, :, cols], preferred_element_type=jnp.float32)
            product = product.reshape(2, number, ROWS, width).astype(jnp.bfloat16)
            part[t, g, slots, :, cols] = product[0]
            pair_out[t, g, slots, :, cols] = product[1]
        remote(pair_out.at[t, g, slots], pair_in.at[t, g, slots], leaving(t, g, PARTIALS),
               arriving(t, g, PAIR_REDUCE + chunk), partner).start()

    def total_of(t, g, block):
        k = SLOT[block]
        total = part[t, g, k].astype(jnp.float32) + pair_in[t, g, k].astype(jnp.float32)
        children = CHILDREN[block]
        if children:
            arrive(t, g, SUMS[block], run_in.at[t, g, pl.ds(0, len(children))])
        for child in children:
            total = total + run_in[t, g, SLOT[child]].astype(jnp.float32)
        return total

    def hand_in(t, g, block):
        k = SLOT[block]
        run_out[t, g, k] = total_of(t, g, block).astype(jnp.bfloat16)
        parent = PARENT[block]
        flip, steps = step_of(block, parent)
        remote(run_out.at[t, g, k], run_in.at[t, g, k], leaving(t, g, SUMMED), arriving(t, g, SUMS[parent]),
               device(p, flip, -steps)).start()

    def store(g):
        return pltpu.make_async_copy(out_v.at[g], outs.at[g], store_sem.at[g])

    def finish(t, g):
        y = (ag[t, g, 0, 0].astype(jnp.float32) + total_of(t, g, (0, 0))).astype(jnp.bfloat16)
        if t + 1 == TICKS:
            out_v[g] = y
            store(g).start()
            return
        if g == 0:
            y_buf[t + 1, 0] = y
            launch_down(t + 1, y_buf.at[t + 1, 0])
        else:
            @pl.when(jnp.logical_not(is_first))
            def _():
                y_buf[t + 1, 1] = y
                launch_up(t + 1, y_buf.at[t + 1, 1])

    def enter(t, g):
        with scope(f"L1_{t}{g}"):
            for block in ((0, 2), (0, 6), (1, 0), (0, 0), (0, 1), (0, 7)):
                take(t, g, block)

    def deepen(t, g):
        with scope(f"L2_{t}{g}"):
            for block in BLOCKS[6:]:
                take(t, g, block)

    def work(t, g, chunk):
        with scope(f"M{chunk}_{t}{g}"):
            multiply(t, g, chunk)

    def leaf(t, g, chunk):
        with scope(f"LV{chunk}_{t}{g}"):
            begin, number = CHUNKS[chunk]
            arrive(t, g, PAIR_REDUCE + chunk, pair_in.at[t, g, pl.ds(begin, number)])
            for block in BLOCKS[begin:begin + number]:
                if block in LEAVES:
                    hand_in(t, g, block)

    def relay(t, g):
        with scope(f"RL_{t}{g}"):
            for block in RELAYS:
                hand_in(t, g, block)

    def close(t, g):
        with scope(f"FI_{t}{g}"):
            finish(t, g)

    def start(g):
        with scope(f"GO_{g}"):
            if g == 0:
                launch_down(0, first.at[0])
            else:
                launch_up(0, first.at[1])

    for copy in loads[:4]:
        copy.wait()
    start(0)
    start(1)
    enter(0, 0)
    enter(0, 1)
    for copy in loads[4:]:
        copy.wait()
    for t in range(TICKS):
        work(t, 0, 0)
        deepen(t, 0)
        if t == 0:
            work(t, 1, 0)
            work(t, 0, 1)
            deepen(t, 1)
        else:
            enter(t, 1)
            work(t, 0, 1)
            work(t, 1, 0)
        leaf(t, 0, 1)
        leaf(t, 0, 0)
        if t > 0:
            deepen(t, 1)
        work(t, 1, 1)
        leaf(t, 1, 0)
        leaf(t, 1, 1)
        relay(t, 0)
        relay(t, 1)
        close(t, 0)
        if t + 1 < TICKS:
            enter(t + 1, 0)
        close(t, 1)
    with scope("drain"):
        for g in range(2):
            store(g).wait()
        for t in range(TICKS):
            for g in range(2):
                for kind, blocks in ((RELAYED, 10), (PAIRED, 16), (PARTIALS, 16), (SUMMED, 15), (LAUNCHED, 5)):
                    ref = ag.at[t, g, 0, pl.ds(0, blocks)]
                    remote(ref, ref, leaving(t, g, kind), arriving(t, g, 0), partner).wait_send()
                ref = ag.at[t, g, 0, 0]
                shift = remote(ref, ref, leaving(t, g, SHIFTED), arriving(t, g, 0), partner)
                pl.when(jnp.logical_not(stays[g]))(shift.wait_send)


def solution(mesh):
    n_pipe = mesh.shape["pipe"]

    def on_device(down_out, up_out, feeds, order, gains, gate_w, up_w, down_w):
        d_model = down_out.shape[-1]
        half = jnp.bfloat16
        anywhere = pl.BlockSpec(memory_space=pl.ANY)
        runs = (TICKS, 2)
        both = pl.pallas_call(
            functools.partial(kernel, n_pipe),
            out_shape=jax.ShapeDtypeStruct((2, ROWS, d_model), half),
            in_specs=[anywhere] * 8,
            out_specs=anywhere,
            scratch_shapes=[
                pltpu.VMEM((2, d_model, 256), half),
                pltpu.VMEM((2, 128, d_model), half),
                pltpu.VMEM((1, 2, d_model), jnp.float32),
                pltpu.VMEM((TICKS, ROWS, d_model), half),
                pltpu.VMEM((2, ROWS, d_model), half),
                pltpu.VMEM(runs + (2, 16, ROWS, d_model), half),
                pltpu.VMEM(runs + (16, ROWS, d_model), half),
                pltpu.VMEM(runs + (16, ROWS, d_model), half),
                pltpu.VMEM(runs + (16, ROWS, d_model), half),
                pltpu.VMEM(runs + (16, ROWS, d_model), half),
                pltpu.VMEM(runs + (16, ROWS, d_model), half),
                pltpu.VMEM(runs + (ROWS, d_model), half),
                pltpu.SMEM((TICKS,), jnp.int32),
                pltpu.VMEM((2, ROWS, d_model), half),
                pltpu.SemaphoreType.DMA((TICKS * 2 * KINDS,)),
                pltpu.SemaphoreType.DMA((TICKS * 2 * ARRIVALS,)),
                pltpu.SemaphoreType.DMA((11,)),
                pltpu.SemaphoreType.DMA((2,)),
            ],
            compiler_params=pltpu.CompilerParams(
                collective_id=0, has_side_effects=True, vmem_limit_bytes=60 * 1024 * 1024),
        )(down_out, up_out, feeds, order, gains, gate_w, up_w, down_w)
        return both[:1], both[1:]

    return jax.shard_map(
        on_device,
        mesh=mesh,
        in_specs=(
            P("pipe", "zero", None),
            P("pipe", "zero", None),
            P(None, "zero", None),
            P(),
            P("pipe", None, None),
            P("pipe", None, None, "zero"),
            P("pipe", None, None, "zero"),
            P("pipe", None, "zero", None),
        ),
        out_specs=(P("pipe", "zero", None), P("pipe", "zero", None)),
        check_vma=False,
    )
```

```python
import functools

import jax
import jax.numpy as jnp
from jax import lax
from jax.experimental import pallas as pl
from jax.experimental.pallas import tpu as pltpu
from jax.sharding import PartitionSpec as P

MESH = pl.DeviceIdType.MESH
TICKS = 2
ROWS = 8

BLOCKS = (
    (0, 0), (0, 1), (0, 7), (0, 2), (0, 6), (1, 0),
    (0, 3), (0, 5), (1, 2), (1, 6), (1, 1),
    (1, 7), (0, 4), (1, 3), (1, 5), (1, 4),
)
CHUNKS = ((0, 6), (6, 10))
SLOT = {block: index for index, block in enumerate(BLOCKS)}
PARENT = {
    (0, 2): (0, 0), (0, 6): (0, 0), (1, 0): (0, 0), (0, 1): (0, 0), (0, 7): (0, 0),
    (1, 3): (0, 2), (0, 4): (0, 2), (1, 2): (0, 2), (0, 3): (0, 2),
    (1, 4): (0, 6), (1, 5): (0, 6), (1, 6): (0, 6), (0, 5): (0, 6),
    (1, 1): (1, 0), (1, 7): (1, 0),
}
CHILDREN = {block: [child for child, parent in PARENT.items() if parent == block] for block in BLOCKS}
RELAYS = [block for block in BLOCKS[1:] if CHILDREN[block]]
LEAVES = [block for block in BLOCKS[1:] if not CHILDREN[block]]

PAIR_GATHER = 16
PAIR_REDUCE = 18
REDUCE = 20
SUMS = {block: REDUCE + index for index, block in enumerate([(0, 0)] + RELAYS)}
ARRIVALS = REDUCE + len(SUMS)
RELAYED, PAIRED, PARTIALS, SUMMED, LAUNCHED, SHIFTED = range(6)
KINDS = 6


def step_of(child, parent):
    return child[0] ^ parent[0], (child[1] - parent[1] + 4) % 8 - 4


def kernel(n_pipe, down_ref, up_ref, feeds_ref, order_hbm, gains_ref, gate_ref, upw_ref, downw_ref,
           outs,
           wgu, wd, gain_v, feed_v, first, ag, part, pair_out, pair_in, run_out, run_in, y_buf,
           order_ref, out_v, send_sem, recv_sem, load_sem, store_sem):
    scope = jax.named_scope
    p = lax.axis_index("pipe")
    q = lax.axis_index("zero")
    d_model = wgu.shape[1]
    opposite = q + 2 - 4 * lax.rem(q // 2, 2)

    def device(plane, flip, steps):
        return (plane, lax.rem((opposite if flip else q) + 4 * (steps % 8), 32))

    partner = (p, q + 1 - 2 * lax.rem(q, 2))
    is_first = p == 0
    is_last = p == n_pipe - 1
    stays = (is_last, is_first)

    loads = []

    def load(src, dst):
        copy = pltpu.make_async_copy(src, dst, load_sem.at[len(loads)])
        copy.start()
        loads.append(copy)

    load(order_hbm, order_ref)
    load(feeds_ref, feed_v)
    load(down_ref.at[0], first.at[0])
    load(up_ref.at[0], first.at[1])
    load(gains_ref, gain_v)
    for g in range(2):
        load(gate_ref.at[0, g], wgu.at[g, :, pl.ds(0, 128)])
        load(upw_ref.at[0, g], wgu.at[g, :, pl.ds(128, 128)])
        load(downw_ref.at[0, g], wd.at[g])

    barrier = pltpu.get_barrier_semaphore()
    near = {step_of(child, parent) for child, parent in PARENT.items()}
    near = sorted(near | {(flip, -steps) for flip, steps in near})
    roots = sorted({(0, 0)} | {step_of(child, (0, 0)) for child in CHILDREN[0, 0]})
    meets = [partner] + [device(p, *step) for step in near]
    barrier_count = len(meets) + jnp.where(is_first, 0, len(roots)) + jnp.where(is_last, 0, len(roots))
    with scope("barr"):
        for other in meets:
            pl.semaphore_signal(barrier, inc=1, device_id=other, device_id_type=MESH)

        @pl.when(jnp.logical_not(is_last))
        def _():
            for step in roots:
                pl.semaphore_signal(barrier, inc=1, device_id=device(p + 1, *step), device_id_type=MESH)

        @pl.when(jnp.logical_not(is_first))
        def _():
            for step in roots:
                pl.semaphore_signal(barrier, inc=1, device_id=device(p - 1, *step), device_id_type=MESH)

        pl.semaphore_wait(barrier, barrier_count)

    def leaving(t, g, kind):
        return send_sem.at[(t * 2 + g) * KINDS + kind]

    def arriving(t, g, number):
        return recv_sem.at[(t * 2 + g) * ARRIVALS + number]

    def remote(src, dst, out_sem, in_sem, device):
        return pltpu.make_async_remote_copy(
            src_ref=src, dst_ref=dst, send_sem=out_sem, recv_sem=in_sem, device_id=device, device_id_type=MESH)

    def arrive(t, g, number, dst):
        remote(dst, dst, leaving(t, g, 0), arriving(t, g, number), partner).wait_recv()

    def place(t, g, block, r=0):
        return ag.at[t, g, r, SLOT[block]]

    def launch(t, stream, src, plane, g, stays):
        for child in CHILDREN[0, 0][:2] + [(0, 0)] + CHILDREN[0, 0][2:]:
            kind = SHIFTED if child == (0, 0) else LAUNCHED
            copy = remote(src, place(t, g, child), leaving(t, stream, kind), arriving(t, g, SLOT[child]),
                          device(plane, *step_of(child, (0, 0))))
            if child == (0, 0):
                pl.when(jnp.logical_not(stays))(copy.start)
                own = pltpu.make_async_copy(src, place(t, g, child), arriving(t, g, SLOT[child]))
                pl.when(stays)(own.start)
            else:
                copy.start()

    def launch_down(t, src):
        launch(t, 0, src, jnp.where(is_last, p, p + 1), jnp.where(is_last, 1, 0), is_last)

        @pl.when(is_first)
        def _():
            y_buf[t, 1] = feed_v[order_ref[t]]
            launch(t, 1, y_buf.at[t, 1], p, 0, is_first)

    def launch_up(t, src):
        @pl.when(jnp.logical_not(is_first))
        def _():
            launch(t, 1, src, p - 1, 1, is_first)

    def take(t, g, block):
        src = place(t, g, block)
        arrive(t, g, SLOT[block], src)
        if block != (0, 0):
            for child in CHILDREN[block]:
                remote(src, place(t, g, child), leaving(t, g, RELAYED), arriving(t, g, SLOT[child]),
                       device(p, *step_of(child, block))).start()
        chunk = sum(SLOT[block] >= begin for begin, _ in CHUNKS) - 1
        remote(src, place(t, g, block, 1), leaving(t, g, PAIRED), arriving(t, g, PAIR_GATHER + chunk), partner).start()

    def multiply(t, g, chunk):
        begin, number = CHUNKS[chunk]
        slots = pl.ds(begin, number)
        arrive(t, g, PAIR_GATHER + chunk, ag.at[t, g, 1, slots])
        x = ag[t, g, :, slots].astype(jnp.float32).reshape(2 * number * ROWS, d_model)
        scale = lax.rsqrt(jnp.mean(x * x, axis=-1, keepdims=True) + 1e-05)
        rows = (x * scale * gain_v[0, pl.ds(g, 1), :]).astype(jnp.bfloat16)
        both = jnp.dot(rows, wgu[g], preferred_element_type=jnp.float32)
        gate = both[:, :128]
        hidden = (gate / (1.0 + jnp.exp(-gate)) * both[:, 128:]).astype(jnp.bfloat16)
        width = min(512, d_model)
        for n in range(d_model // width):
            cols = pl.ds(n * width, width)
            product = jnp.dot(hidden, wd[g, :, cols], preferred_element_type=jnp.float32)
            product = product.reshape(2, number, ROWS, width).astype(jnp.bfloat16)
            part[t, g, slots, :, cols] = product[0]
            pair_out[t, g, slots, :, cols] = product[1]
        remote(pair_out.at[t, g, slots], pair_in.at[t, g, slots], leaving(t, g, PARTIALS),
               arriving(t, g, PAIR_REDUCE + chunk), partner).start()

    def total_of(t, g, block):
        k = SLOT[block]
        total = part[t, g, k].astype(jnp.float32) + pair_in[t, g, k].astype(jnp.float32)
        children = CHILDREN[block]
        if children:
            arrive(t, g, SUMS[block], run_in.at[t, g, pl.ds(0, len(children))])
        for child in children:
            total = total + run_in[t, g, SLOT[child]].astype(jnp.float32)
        return total

    def hand_in(t, g, block):
        k = SLOT[block]
        run_out[t, g, k] = total_of(t, g, block).astype(jnp.bfloat16)
        parent = PARENT[block]
        flip, steps = step_of(block, parent)
        remote(run_out.at[t, g, k], run_in.at[t, g, k], leaving(t, g, SUMMED), arriving(t, g, SUMS[parent]),
               device(p, flip, -steps)).start()

    def store(g):
        return pltpu.make_async_copy(out_v.at[g], outs.at[g], store_sem.at[g])

    def finish(t, g):
        y = (ag[t, g, 0, 0].astype(jnp.float32) + total_of(t, g, (0, 0))).astype(jnp.bfloat16)
        if t + 1 == TICKS:
            out_v[g] = y
            store(g).start()
            return
        if g == 0:
            y_buf[t + 1, 0] = y
            launch_down(t + 1, y_buf.at[t + 1, 0])
        else:
            @pl.when(jnp.logical_not(is_first))
            def _():
                y_buf[t + 1, 1] = y
                launch_up(t + 1, y_buf.at[t + 1, 1])

    def enter(t, g):
        with scope(f"L1_{t}{g}"):
            for block in ((0, 2), (0, 6), (1, 0), (0, 0), (0, 1), (0, 7)):
                take(t, g, block)

    def deepen(t, g):
        with scope(f"L2_{t}{g}"):
            for block in BLOCKS[6:]:
                take(t, g, block)

    def work(t, g, chunk):
        with scope(f"M{chunk}_{t}{g}"):
            multiply(t, g, chunk)

    def leaf(t, g, chunk):
        with scope(f"LV{chunk}_{t}{g}"):
            begin, number = CHUNKS[chunk]
            arrive(t, g, PAIR_REDUCE + chunk, pair_in.at[t, g, pl.ds(begin, number)])
            for block in reversed(BLOCKS[begin:begin + number]):
                if block in LEAVES:
                    hand_in(t, g, block)

    def relay(t, g):
        with scope(f"RL_{t}{g}"):
            for block in RELAYS:
                hand_in(t, g, block)

    def close(t, g):
        with scope(f"FI_{t}{g}"):
            finish(t, g)

    def start(g):
        with scope(f"GO_{g}"):
            if g == 0:
                launch_down(0, first.at[0])
            else:
                launch_up(0, first.at[1])

    for copy in loads[:4]:
        copy.wait()
    start(0)
    start(1)
    enter(0, 0)
    enter(0, 1)
    for copy in loads[4:]:
        copy.wait()
    for t in range(TICKS):
        work(t, 0, 0)
        deepen(t, 0)
        if t == 0:
            work(t, 1, 0)
            work(t, 0, 1)
            deepen(t, 1)
        else:
            enter(t, 1)
            work(t, 0, 1)
            work(t, 1, 0)
        leaf(t, 0, 1)
        leaf(t, 0, 0)
        if t > 0:
            deepen(t, 1)
        work(t, 1, 1)
        leaf(t, 1, 0)
        leaf(t, 1, 1)
        relay(t, 0)
        relay(t, 1)
        close(t, 0)
        if t + 1 < TICKS:
            enter(t + 1, 0)
        close(t, 1)
    with scope("drain"):
        for g in range(2):
            store(g).wait()
        for t in range(TICKS):
            for g in range(2):
                for kind, blocks in ((RELAYED, 10), (PAIRED, 16), (PARTIALS, 16), (SUMMED, 15), (LAUNCHED, 5)):
                    ref = ag.at[t, g, 0, pl.ds(0, blocks)]
                    remote(ref, ref, leaving(t, g, kind), arriving(t, g, 0), partner).wait_send()
                ref = ag.at[t, g, 0, 0]
                shift = remote(ref, ref, leaving(t, g, SHIFTED), arriving(t, g, 0), partner)
                pl.when(jnp.logical_not(stays[g]))(shift.wait_send)


def solution(mesh):
    n_pipe = mesh.shape["pipe"]

    def on_device(down_out, up_out, feeds, order, gains, gate_w, up_w, down_w):
        d_model = down_out.shape[-1]
        half = jnp.bfloat16
        anywhere = pl.BlockSpec(memory_space=pl.ANY)
        runs = (TICKS, 2)
        both = pl.pallas_call(
            functools.partial(kernel, n_pipe),
            out_shape=jax.ShapeDtypeStruct((2, ROWS, d_model), half),
            in_specs=[anywhere] * 8,
            out_specs=anywhere,
            scratch_shapes=[
                pltpu.VMEM((2, d_model, 256), half),
                pltpu.VMEM((2, 128, d_model), half),
                pltpu.VMEM((1, 2, d_model), jnp.float32),
                pltpu.VMEM((TICKS, ROWS, d_model), half),
                pltpu.VMEM((2, ROWS, d_model), half),
                pltpu.VMEM(runs + (2, 16, ROWS, d_model), half),
                pltpu.VMEM(runs + (16, ROWS, d_model), half),
                pltpu.VMEM(runs + (16, ROWS, d_model), half),
                pltpu.VMEM(runs + (16, ROWS, d_model), half),
                pltpu.VMEM(runs + (16, ROWS, d_model), half),
                pltpu.VMEM(runs + (16, ROWS, d_model), half),
                pltpu.VMEM(runs + (ROWS, d_model), half),
                pltpu.SMEM((TICKS,), jnp.int32),
                pltpu.VMEM((2, ROWS, d_model), half),
                pltpu.SemaphoreType.DMA((TICKS * 2 * KINDS,)),
                pltpu.SemaphoreType.DMA((TICKS * 2 * ARRIVALS,)),
                pltpu.SemaphoreType.DMA((11,)),
                pltpu.SemaphoreType.DMA((2,)),
            ],
            compiler_params=pltpu.CompilerParams(
                collective_id=0, has_side_effects=True, vmem_limit_bytes=60 * 1024 * 1024),
        )(down_out, up_out, feeds, order, gains, gate_w, up_w, down_w)
        return both[:1], both[1:]

    return jax.shard_map(
        on_device,
        mesh=mesh,
        in_specs=(
            P("pipe", "zero", None),
            P("pipe", "zero", None),
            P(None, "zero", None),
            P(),
            P("pipe", None, None),
            P("pipe", None, None, "zero"),
            P("pipe", None, None, "zero"),
            P("pipe", None, "zero", None),
        ),
        out_specs=(P("pipe", "zero", None), P("pipe", "zero", None)),
        check_vma=False,
    )
```

```python
import functools

import jax
import jax.numpy as jnp
from jax import lax
from jax.experimental import pallas as pl
from jax.experimental.pallas import tpu as pltpu
from jax.sharding import PartitionSpec as P

MESH = pl.DeviceIdType.MESH
TICKS = 2
ROWS = 8

BLOCKS = (
    (0, 0), (0, 1), (0, 7), (0, 2), (0, 6), (1, 0),
    (0, 3), (0, 5), (1, 2), (1, 6), (1, 1),
    (1, 7), (0, 4), (1, 3), (1, 5), (1, 4),
)
CHUNKS = ((0, 6), (6, 10))
SLOT = {block: index for index, block in enumerate(BLOCKS)}
PARENT = {
    (0, 2): (0, 0), (0, 6): (0, 0), (1, 0): (0, 0), (0, 1): (0, 0), (0, 7): (0, 0),
    (1, 3): (0, 2), (0, 4): (0, 2), (1, 2): (0, 2), (0, 3): (0, 2),
    (1, 4): (0, 6), (1, 5): (0, 6), (1, 6): (0, 6), (0, 5): (0, 6),
    (1, 1): (1, 0), (1, 7): (1, 0),
}
CHILDREN = {block: [child for child, parent in PARENT.items() if parent == block] for block in BLOCKS}
RELAYS = [block for block in BLOCKS[1:] if CHILDREN[block]]
LEAVES = [block for block in BLOCKS[1:] if not CHILDREN[block]]

PAIR_GATHER = 16
PAIR_REDUCE = 18
REDUCE = 20
SUMS = {block: REDUCE + index for index, block in enumerate([(0, 0)] + RELAYS)}
ARRIVALS = REDUCE + len(SUMS)
RELAYED, PAIRED, PARTIALS, SUMMED, LAUNCHED, SHIFTED = range(6)
KINDS = 6


def step_of(child, parent):
    return child[0] ^ parent[0], (child[1] - parent[1] + 4) % 8 - 4


def kernel(n_pipe, down_ref, up_ref, feeds_ref, order_hbm, gains_ref, gate_ref, upw_ref, downw_ref,
           outs,
           wgu, wd, gain_v, feed_v, first, ag, part, pair_out, pair_in, run_out, run_in, y_buf,
           order_ref, out_v, send_sem, recv_sem, load_sem, store_sem):
    scope = jax.named_scope
    p = lax.axis_index("pipe")
    q = lax.axis_index("zero")
    d_model = wgu.shape[1]
    opposite = q + 2 - 4 * lax.rem(q // 2, 2)

    def device(plane, flip, steps):
        return (plane, lax.rem((opposite if flip else q) + 4 * (steps % 8), 32))

    partner = (p, q + 1 - 2 * lax.rem(q, 2))
    is_first = p == 0
    is_last = p == n_pipe - 1
    stays = (is_last, is_first)

    loads = []

    def load(src, dst):
        copy = pltpu.make_async_copy(src, dst, load_sem.at[len(loads)])
        copy.start()
        loads.append(copy)

    load(order_hbm, order_ref)
    load(feeds_ref, feed_v)
    load(down_ref.at[0], first.at[0])
    load(up_ref.at[0], first.at[1])
    load(gains_ref, gain_v)
    for g in range(2):
        load(gate_ref.at[0, g], wgu.at[g, :, pl.ds(0, 128)])
        load(upw_ref.at[0, g], wgu.at[g, :, pl.ds(128, 128)])
        load(downw_ref.at[0, g], wd.at[g])

    barrier = pltpu.get_barrier_semaphore()
    near = {step_of(child, parent) for child, parent in PARENT.items()}
    near = sorted(near | {(flip, -steps) for flip, steps in near})
    roots = sorted({(0, 0)} | {step_of(child, (0, 0)) for child in CHILDREN[0, 0]})
    meets = [partner] + [device(p, *step) for step in near]
    barrier_count = len(meets) + jnp.where(is_first, 0, len(roots)) + jnp.where(is_last, 0, len(roots))
    with scope("barr"):
        for other in meets:
            pl.semaphore_signal(barrier, inc=1, device_id=other, device_id_type=MESH)

        @pl.when(jnp.logical_not(is_last))
        def _():
            for step in roots:
                pl.semaphore_signal(barrier, inc=1, device_id=device(p + 1, *step), device_id_type=MESH)

        @pl.when(jnp.logical_not(is_first))
        def _():
            for step in roots:
                pl.semaphore_signal(barrier, inc=1, device_id=device(p - 1, *step), device_id_type=MESH)

        pl.semaphore_wait(barrier, barrier_count)

    def leaving(t, g, kind):
        return send_sem.at[(t * 2 + g) * KINDS + kind]

    def arriving(t, g, number):
        return recv_sem.at[(t * 2 + g) * ARRIVALS + number]

    def remote(src, dst, out_sem, in_sem, device):
        return pltpu.make_async_remote_copy(
            src_ref=src, dst_ref=dst, send_sem=out_sem, recv_sem=in_sem, device_id=device, device_id_type=MESH)

    def arrive(t, g, number, dst):
        remote(dst, dst, leaving(t, g, 0), arriving(t, g, number), partner).wait_recv()

    def place(t, g, block, r=0):
        return ag.at[t, g, r, SLOT[block]]

    def launch(t, stream, src, plane, g, stays):
        for child in CHILDREN[0, 0][:2] + [(0, 0)] + CHILDREN[0, 0][2:]:
            kind = SHIFTED if child == (0, 0) else LAUNCHED
            copy = remote(src, place(t, g, child), leaving(t, stream, kind), arriving(t, g, SLOT[child]),
                          device(plane, *step_of(child, (0, 0))))
            if child == (0, 0):
                pl.when(jnp.logical_not(stays))(copy.start)
                own = pltpu.make_async_copy(src, place(t, g, child), arriving(t, g, SLOT[child]))
                pl.when(stays)(own.start)
            else:
                copy.start()

    def launch_down(t, src):
        launch(t, 0, src, jnp.where(is_last, p, p + 1), jnp.where(is_last, 1, 0), is_last)

        @pl.when(is_first)
        def _():
            y_buf[t, 1] = feed_v[order_ref[t]]
            launch(t, 1, y_buf.at[t, 1], p, 0, is_first)

    def launch_up(t, src):
        @pl.when(jnp.logical_not(is_first))
        def _():
            launch(t, 1, src, p - 1, 1, is_first)

    def take(t, g, block):
        src = place(t, g, block)
        arrive(t, g, SLOT[block], src)
        if block != (0, 0):
            for child in CHILDREN[block]:
                remote(src, place(t, g, child), leaving(t, g, RELAYED), arriving(t, g, SLOT[child]),
                       device(p, *step_of(child, block))).start()
        chunk = sum(SLOT[block] >= begin for begin, _ in CHUNKS) - 1
        remote(src, place(t, g, block, 1), leaving(t, g, PAIRED), arriving(t, g, PAIR_GATHER + chunk), partner).start()

    def multiply(t, g, chunk):
        begin, number = CHUNKS[chunk]
        slots = pl.ds(begin, number)
        arrive(t, g, PAIR_GATHER + chunk, ag.at[t, g, 1, slots])
        x = ag[t, g, :, slots].astype(jnp.float32).reshape(2 * number * ROWS, d_model)
        scale = lax.rsqrt(jnp.mean(x * x, axis=-1, keepdims=True) + 1e-05)
        rows = (x * scale * gain_v[0, pl.ds(g, 1), :]).astype(jnp.bfloat16)
        both = jnp.dot(rows, wgu[g], preferred_element_type=jnp.float32)
        gate = both[:, :128]
        hidden = (gate / (1.0 + jnp.exp(-gate)) * both[:, 128:]).astype(jnp.bfloat16)
        width = min(512, d_model)
        for n in range(d_model // width):
            cols = pl.ds(n * width, width)
            product = jnp.dot(hidden, wd[g, :, cols], preferred_element_type=jnp.float32)
            product = product.reshape(2, number, ROWS, width).astype(jnp.bfloat16)
            part[t, g, slots, :, cols] = product[0]
            pair_out[t, g, slots, :, cols] = product[1]
        remote(pair_out.at[t, g, slots], pair_in.at[t, g, slots], leaving(t, g, PARTIALS),
               arriving(t, g, PAIR_REDUCE + chunk), partner).start()

    def total_of(t, g, block):
        k = SLOT[block]
        total = part[t, g, k].astype(jnp.float32) + pair_in[t, g, k].astype(jnp.float32)
        children = CHILDREN[block]
        if children:
            arrive(t, g, SUMS[block], run_in.at[t, g, pl.ds(0, len(children))])
        for child in children:
            total = total + run_in[t, g, SLOT[child]].astype(jnp.float32)
        return total

    def hand_in(t, g, block):
        k = SLOT[block]
        run_out[t, g, k] = total_of(t, g, block).astype(jnp.bfloat16)
        parent = PARENT[block]
        flip, steps = step_of(block, parent)
        remote(run_out.at[t, g, k], run_in.at[t, g, k], leaving(t, g, SUMMED), arriving(t, g, SUMS[parent]),
               device(p, flip, -steps)).start()

    def store(g):
        return pltpu.make_async_copy(out_v.at[g], outs.at[g], store_sem.at[g])

    def finish(t, g):
        y = (ag[t, g, 0, 0].astype(jnp.float32) + total_of(t, g, (0, 0))).astype(jnp.bfloat16)
        if t + 1 == TICKS:
            out_v[g] = y
            store(g).start()
            return
        if g == 0:
            y_buf[t + 1, 0] = y
            launch_down(t + 1, y_buf.at[t + 1, 0])
        else:
            @pl.when(jnp.logical_not(is_first))
            def _():
                y_buf[t + 1, 1] = y
                launch_up(t + 1, y_buf.at[t + 1, 1])

    def enter(t, g):
        with scope(f"L1_{t}{g}"):
            for block in ((0, 2), (0, 6), (1, 0), (0, 0), (0, 1), (0, 7)):
                take(t, g, block)

    def deepen(t, g):
        with scope(f"L2_{t}{g}"):
            for block in ((0, 3), (0, 5), (1, 1), (1, 7), (1, 2), (1, 6), (0, 4), (1, 3), (1, 5), (1, 4)):
                take(t, g, block)

    def work(t, g, chunk):
        with scope(f"M{chunk}_{t}{g}"):
            multiply(t, g, chunk)

    def leaf(t, g, chunk):
        with scope(f"LV{chunk}_{t}{g}"):
            begin, number = CHUNKS[chunk]
            arrive(t, g, PAIR_REDUCE + chunk, pair_in.at[t, g, pl.ds(begin, number)])
            for block in reversed(BLOCKS[begin:begin + number]):
                if block in LEAVES:
                    hand_in(t, g, block)

    def relay(t, g):
        with scope(f"RL_{t}{g}"):
            for block in RELAYS:
                hand_in(t, g, block)

    def close(t, g):
        with scope(f"FI_{t}{g}"):
            finish(t, g)

    def start(g):
        with scope(f"GO_{g}"):
            if g == 0:
                launch_down(0, first.at[0])
            else:
                launch_up(0, first.at[1])

    for copy in loads[:4]:
        copy.wait()
    start(0)
    start(1)
    enter(0, 0)
    enter(0, 1)
    for copy in loads[4:]:
        copy.wait()
    for t in range(TICKS):
        work(t, 0, 0)
        deepen(t, 0)
        if t == 0:
            work(t, 1, 0)
            work(t, 0, 1)
            deepen(t, 1)
        else:
            enter(t, 1)
            work(t, 0, 1)
            work(t, 1, 0)
        leaf(t, 0, 1)
        leaf(t, 0, 0)
        if t > 0:
            deepen(t, 1)
        work(t, 1, 1)
        leaf(t, 1, 0)
        leaf(t, 1, 1)
        relay(t, 0)
        close(t, 0)
        relay(t, 1)
        if t + 1 < TICKS:
            enter(t + 1, 0)
        close(t, 1)
    with scope("drain"):
        for g in range(2):
            store(g).wait()
        for t in range(TICKS):
            for g in range(2):
                for kind, blocks in ((RELAYED, 10), (PAIRED, 16), (PARTIALS, 16), (SUMMED, 15), (LAUNCHED, 5)):
                    ref = ag.at[t, g, 0, pl.ds(0, blocks)]
                    remote(ref, ref, leaving(t, g, kind), arriving(t, g, 0), partner).wait_send()
                ref = ag.at[t, g, 0, 0]
                shift = remote(ref, ref, leaving(t, g, SHIFTED), arriving(t, g, 0), partner)
                pl.when(jnp.logical_not(stays[g]))(shift.wait_send)


def solution(mesh):
    n_pipe = mesh.shape["pipe"]

    def on_device(down_out, up_out, feeds, order, gains, gate_w, up_w, down_w):
        d_model = down_out.shape[-1]
        half = jnp.bfloat16
        anywhere = pl.BlockSpec(memory_space=pl.ANY)
        runs = (TICKS, 2)
        both = pl.pallas_call(
            functools.partial(kernel, n_pipe),
            out_shape=jax.ShapeDtypeStruct((2, ROWS, d_model), half),
            in_specs=[anywhere] * 8,
            out_specs=anywhere,
            scratch_shapes=[
                pltpu.VMEM((2, d_model, 256), half),
                pltpu.VMEM((2, 128, d_model), half),
                pltpu.VMEM((1, 2, d_model), jnp.float32),
                pltpu.VMEM((TICKS, ROWS, d_model), half),
                pltpu.VMEM((2, ROWS, d_model), half),
                pltpu.VMEM(runs + (2, 16, ROWS, d_model), half),
                pltpu.VMEM(runs + (16, ROWS, d_model), half),
                pltpu.VMEM(runs + (16, ROWS, d_model), half),
                pltpu.VMEM(runs + (16, ROWS, d_model), half),
                pltpu.VMEM(runs + (16, ROWS, d_model), half),
                pltpu.VMEM(runs + (16, ROWS, d_model), half),
                pltpu.VMEM(runs + (ROWS, d_model), half),
                pltpu.SMEM((TICKS,), jnp.int32),
                pltpu.VMEM((2, ROWS, d_model), half),
                pltpu.SemaphoreType.DMA((TICKS * 2 * KINDS,)),
                pltpu.SemaphoreType.DMA((TICKS * 2 * ARRIVALS,)),
                pltpu.SemaphoreType.DMA((11,)),
                pltpu.SemaphoreType.DMA((2,)),
            ],
            compiler_params=pltpu.CompilerParams(
                collective_id=0, has_side_effects=True, vmem_limit_bytes=60 * 1024 * 1024),
        )(down_out, up_out, feeds, order, gains, gate_w, up_w, down_w)
        return both[:1], both[1:]

    return jax.shard_map(
        on_device,
        mesh=mesh,
        in_specs=(
            P("pipe", "zero", None),
            P("pipe", "zero", None),
            P(None, "zero", None),
            P(),
            P("pipe", None, None),
            P("pipe", None, None, "zero"),
            P("pipe", None, None, "zero"),
            P("pipe", None, "zero", None),
        ),
        out_specs=(P("pipe", "zero", None), P("pipe", "zero", None)),
        check_vma=False,
    )
```
